256 devices in a mesh: band: 4 (over x), grid: 64 (over z, y, core).
Axes of the slice: x: 4, y: 4, z: 8, core: 2. Of those that a mesh axis runs over, the one named last changes fastest.
Arguments:
- orbitals: float32 [256, 512, 1024], P('band', 'grid'), may hold values from -6 to 6
- potentials: bfloat16 [2048, 512, 1024], P(None, 'grid', 'band'), may hold values from -0.0078125 to 0.0078125
- point_rows: int32 [2048], replicated, may hold values from 0 to 511
- point_cols: int32 [2048], replicated, may hold values from 0 to 1023
Outputs:
- exchanged: float32 [256, 512, 1024], P('band', 'grid')
The draws below stay inside these ranges and needn't reach their ends.
All inputs are finite; a program needn't handle non-finite values.
Results may differ from the reference program's by a relative error of at most 0.0003.
Values sent between devices are 32-bit elements; how exact they have to be, the bound alone decides.
A program may use at most 128 MiB of HBM per device.

```python
import math
import jax
import jax.numpy as jnp
import numpy as np
from jax import lax

NB = 256
NP = 2048
NC = 1024
NR = 512


def with_ends(values, key, low, top_value):
    place = [jax.random.randint(jax.random.fold_in(key, axis), (), 0, length) for axis, length in enumerate(values.shape)]
    longest = values.shape.index(max(values.shape))
    neighbour = place[:longest] + [(place[longest] + 1) % values.shape[longest]] + place[longest + 1:]
    return values.at[tuple(place)].set(low).at[tuple(neighbour)].set(top_value)


def levels(key, shape, split, low, high):
    level, own = 1.0, jax.random.fold_in(key, 6)
    for dim, shards_of in split:
        heights = jnp.exp(jax.random.uniform(jax.random.fold_in(own, dim), (shards_of,), jnp.float32, low / len(split), high / len(split)))
        level = level * jnp.repeat(heights, shape[dim] // shards_of).reshape([-1 if axis == dim else 1 for axis in range(len(shape))])
    return level


def rank_table(amount, skew):
    weights = [(1 << 20) // math.isqrt(rank ** skew) + 1 for rank in range(1, amount + 1)]
    scale = 1 + sum(weights) // (1 << 30)
    return np.cumsum(np.array([max(1, weight // scale) for weight in weights]))


def ranked(key, extent, number_of, skew):
    listing = rank_table(number_of, skew)
    pick = jax.random.randint(jax.random.fold_in(key, 1), extent, 0, int(listing[number_of - 1]))
    grade = jnp.searchsorted(jnp.asarray(listing, jnp.int32), pick, side="right")
    return jax.random.permutation(jax.random.fold_in(key, 2), number_of)[grade].astype(jnp.int32)


def gaussian(key, dims, deviation, limit, cuts=(), kind=jnp.bfloat16):
    array = deviation * jax.random.normal(key, dims, jnp.float32)
    if cuts:
        array = array * levels(key, dims, cuts, -0.22, 0.18)
    return jnp.clip(array, -limit, limit).astype(kind)


def setup_inputs(seed: int = 0) -> dict:
    splits = jax.random.split(jax.random.key(seed), 5)
    orbitals = gaussian(splits[0], (NB, NR, NC), 1.0, 6.0, ((0, 4), (1, 64)), jnp.float32)
    potentials = gaussian(splits[1], (NP, NR, NC), (NB * NP) ** -0.5, 0.0078125, ((1, 64), (2, 4)))
    point_rows = with_ends(ranked(splits[2], (NP,), NR, 2), jax.random.fold_in(splits[2], 3), 0, NR - 1).astype(jnp.int32)
    point_cols = with_ends(jax.random.randint(splits[3], (NP,), 0, NC), jax.random.fold_in(splits[3], 1), 0, NC - 1).astype(jnp.int32)
    return dict(orbitals=orbitals, potentials=potentials, point_rows=point_rows, point_cols=point_cols)


def reference(orbitals, potentials, point_rows, point_cols):
    point_panel = orbitals[:, point_rows, point_cols]

    def one_row(index):
        row_block = orbitals[:, index, :]
        kernel = jnp.dot(point_panel.T, row_block, precision=lax.Precision.HIGHEST, preferred_element_type=jnp.float32)
        weighted = kernel * potentials[:, index, :].astype(jnp.float32)
        return -jnp.dot(point_panel, weighted, precision=lax.Precision.HIGHEST, preferred_element_type=jnp.float32)

    rows_out = lax.map(one_row, jnp.arange(NR, dtype=jnp.int32))
    return jnp.transpose(rows_out, (1, 0, 2))
```

```python
import jax
import jax.numpy as jnp
from jax import lax
from jax.experimental import pallas as pl
from jax.experimental.pallas import tpu as pltpu
from jax.sharding import PartitionSpec as P

MESH = pl.DeviceIdType.MESH
BF = jnp.bfloat16
F32 = jnp.float32
MC = 512


def split(v):
    hi = v.astype(BF)
    return hi, (v - hi.astype(F32)).astype(BF)


def body(orb, pot, rows, cols, y_out,
         orbv, vraw, vrow, amat, orecv, ohi, olo, qa, ra, qb, rb, qc, rc, qd, rd,
         pt, pth, ptl, ph, plo, ysend,
         lsem, in_s, in_r, a_s, a_r, b_s, b_r, c_s, c_r, d_s, d_r,
         z_s, z_r, y_s, y_r, k_s, k_r, o_s, o_r, o_l):
    x = lax.axis_index("band")
    g = lax.axis_index("grid")
    z, y, c = g // 8, (g // 2) % 4, g % 2

    def dev(xx, zz, yy, cc):
        return (xx, (zz * 4 + yy) * 2 + cc)

    def xpeer(d):
        return dev((x + d) % 4, z, y, c)

    def zpeer(d):
        return dev(x, (z + d) % 8, y, c)

    def ypeer(d):
        return dev(x, z, (y + d) % 4, c)

    partner = dev(x, z, y, 1 - c)

    def remote(src, dst, ss, rs, to):
        return pltpu.make_async_remote_copy(
            src_ref=src, dst_ref=dst, send_sem=ss, recv_sem=rs,
            device_id=to, device_id_type=MESH)

    load_orb = [pltpu.make_async_copy(orb.at[:, pl.ds(128 * t, 128)], orbv.at[t], lsem.at[t])
                for t in range(8)]
    for cp in load_orb:
        cp.start()
    load_pot = pltpu.make_async_copy(pot, vraw, lsem.at[10])
    load_pot.start()

    def columns(to, t):
        return orb.at[:, pl.ds(pl.multiple_of(256 * to + 128 * t, 128), 128)]

    def landing(t):
        return orecv.at[t, pl.ds(pl.multiple_of(512 * x, 512), 512), :]

    load_own = [pltpu.make_async_copy(columns(x, t), landing(t), lsem.at[8 + t]) for t in range(2)]
    for cp in load_own:
        cp.start()

    barrier = pltpu.get_barrier_semaphore()
    peers = ([partner] + [xpeer(d) for d in (1, 2, 3)] + [ypeer(d) for d in (1, 2, 3)]
             + [zpeer(d) for d in range(1, 8)])
    for to in peers:
        pl.semaphore_signal(barrier, inc=1, device_id=to, device_id_type=MESH)

    for t in range(8):
        load_orb[t].wait()
        at = pl.ds(128 * t, 128)
        for r in range(8):
            hi, lo = split(orbv[t, pl.ds(r, 64, stride=8), :])
            amat[pl.ds(64 * r, 64), at] = hi
            amat[pl.ds(512 + 64 * r, 64), at] = lo

    def pick(b):
        at = pl.ds(pl.multiple_of(256 * b, 256), 256)
        hot = lax.broadcasted_iota(jnp.int32, (1024, 256), 0) == cols[:, at]
        res = jnp.dot(amat[...], jnp.where(hot, 1.0, 0.0).astype(BF), preferred_element_type=F32)
        here = rows[:, at] - 8 * g
        total = jnp.zeros((64, 256), F32)
        for r in range(8):
            part = res[64 * r:64 * r + 64] + res[512 + 64 * r:576 + 64 * r]
            total = total + jnp.where(here == r, part, 0.0)
        return jnp.concatenate([total[:, :128], total[:, 128:]], axis=0).T

    def inbound(d, part):
        return remote(
            columns((x + d) % 4, part), landing(part), in_s.at[part, d - 1], in_r.at[part, d - 1], xpeer(d))

    acopies = []
    for i in range(4):
        qa[i] = pick((1 - c) * 4 + (y + 1 + i) % 4)
        if i == 0:
            pl.semaphore_wait(barrier, len(peers))
            for d in (1, 3, 2):
                inbound(d, 0).start()
        acopies.append(remote(qa.at[i], ra.at[i], a_s.at[i], a_r.at[i], partner))
        acopies[i].start()
    bcopies = []
    for i in range(4):
        mine = pick(c * 4 + (y + 1 + i) % 4)
        acopies[i].wait_recv()
        qb[i] = mine + ra[i]
        if i < 3:
            bcopies.append(remote(qb.at[i], rb.at[i], b_s.at[i], b_r.at[i], ypeer(i + 1)))
            bcopies[i].start()

    def rearrange(start, stop):
        @pl.loop(start, stop)
        def _(n):
            at = pl.ds(pl.multiple_of(16 * n, 16), 16)
            v = vraw[at, :, :].astype(F32)
            vrow[:, at, :] = jnp.swapaxes(v, 0, 1).astype(BF)

    load_pot.wait()
    rearrange(0, 32)
    for cp in bcopies:
        cp.wait_recv()
    qc[...] = qb[3] + rb[0] + rb[1] + rb[2]
    ccopies = []
    for d in range(1, 8):
        to = (z + d) % 8
        ccopies.append(remote(qc.at[pl.ds(pl.multiple_of(16 * to, 16), 16), :], rc.at[d - 1],
                              c_s.at[d - 1], c_r.at[d - 1], zpeer(d)))
        ccopies[-1].start()
    rearrange(32, 64)
    total = qc[pl.ds(pl.multiple_of(16 * z, 16), 16), :]
    for d in range(1, 8):
        ccopies[d - 1].wait_recv()
        total = total + rc[d - 1]
    qd[...] = total
    dcopies = []
    for d in (1, 2, 3):
        dcopies.append(remote(qd, rd.at[d - 1], d_s.at[d - 1], d_r.at[d - 1], xpeer(d)))
        dcopies[-1].start()
    for d in (1, 3, 2):
        inbound(d, 1).start()
    rearrange(64, 80)
    for cp in dcopies:
        cp.wait_recv()
    lane = lax.broadcasted_iota(jnp.int32, (16, 128), 1)
    low = lane < 64
    halves = []
    for d in range(4):
        q = qd[...] if d == 0 else rd[d - 1]
        other = pltpu.roll(q, 64, 1)
        halves.append((jnp.where(low, q, other), jnp.where(low, other, q)))
    b = c * 4 + y
    for h in range(2):
        for t in range(2):
            v = jnp.zeros((16, 128), F32)
            for d in range(4):
                v = v + jnp.where(lane // 64 + 2 * t == (x + 4 - d) % 4, halves[d][h], 0.0)
            pt[2 * b + h, pl.ds(pl.multiple_of(16 * z, 16), 16), pl.ds(128 * t, 128)] = v

    def zpiece():
        return pt.at[pl.ds(2 * b, 2), pl.ds(pl.multiple_of(16 * z, 16), 16), :]

    zcopies = []
    for d in range(1, 8):
        zcopies.append(remote(zpiece(), zpiece(), z_s.at[d - 1], z_r.at[d - 1], zpeer(d)))
        zcopies[-1].start()
    rearrange(80, 112)
    for cp in zcopies:
        cp.wait_recv()

    def block(bb):
        return pt.at[pl.ds(2 * bb, 2)]

    ycopies, kcopies = [], []
    for d in (1, 3, 2):
        ycopies.append(remote(block(b), block(b), y_s.at[d - 1], y_r.at[d - 1], ypeer(d)))
        ycopies[-1].start()
    kcopies.append(remote(block(b), block(b), k_s.at[0], k_r.at[0], partner))
    kcopies[0].start()
    rearrange(112, 128)
    for cp in load_own:
        cp.wait()
    for part in range(2):
        for d in (1, 2, 3):
            inbound(d, part).wait_recv()
    for r in range(8):
        for t in range(2):
            hi, lo = split(orecv[t, pl.ds(r, 256, stride=8), :])
            ohi[r, :, pl.ds(128 * t, 128)] = hi
            olo[r, :, pl.ds(128 * t, 128)] = lo
    for n, d in enumerate((1, 3, 2)):
        ycopies[n].wait_recv()
        src = c * 4 + (y + 4 - d) % 4
        kcopies.append(remote(block(src), block(src), k_s.at[d], k_r.at[d], partner))
        kcopies[-1].start()
    for cp in kcopies:
        cp.wait_recv()

    eye = jnp.where(lax.broadcasted_iota(jnp.int32, (256, 256), 0)
                    == lax.broadcasted_iota(jnp.int32, (256, 256), 1), 1.0, 0.0).astype(BF)
    nt = (((1,), (1,)), ((), ()))
    for n in range(8):
        at = pl.ds(256 * n, 256)
        hi, lo = split(pt[2 * n:2 * n + 2].reshape(256, 256))
        pth[at, :] = hi
        ptl[at, :] = lo
        ph[:, at] = lax.dot_general(eye, hi, nt, preferred_element_type=F32).astype(BF)
        plo[:, at] = lax.dot_general(eye, lo, nt, preferred_element_type=F32).astype(BF)

    def outbound(r, d):
        to = (x + d) % 4
        return remote(
            ysend.at[r, pl.ds(pl.multiple_of(64 * to, 64), 64), :],
            y_out.at[r, :, pl.ds(pl.multiple_of(256 * x, 256), 256)],
            o_s.at[r, d - 1], o_r.at[r, d - 1], xpeer(d))

    def keep(r):
        return pltpu.make_async_copy(
            ysend.at[r, pl.ds(pl.multiple_of(64 * x, 64), 64), :],
            y_out.at[r, :, pl.ds(pl.multiple_of(256 * x, 256), 256)], o_l.at[r])

    @pl.loop(0, 8)
    def _(r):
        oh, ol = ohi[r], olo[r]
        acc = jnp.zeros((256, 256), F32)
        for n in range(2048 // MC):
            at = pl.ds(MC * n, MC)
            kern = (jnp.dot(pth[at, :], oh, preferred_element_type=F32)
                    + jnp.dot(ptl[at, :], oh, preferred_element_type=F32)
                    + jnp.dot(pth[at, :], ol, preferred_element_type=F32))
            wh, wl = split(kern * vrow[r, at, :].astype(F32))
            acc = (acc + jnp.dot(ph[:, at], wh, preferred_element_type=F32)
                   + jnp.dot(plo[:, at], wh, preferred_element_type=F32)
                   + jnp.dot(ph[:, at], wl, preferred_element_type=F32))
        ysend[r] = -acc
        for d in (1, 3, 2):
            outbound(r, d).start()
        keep(r).start()

    for part in range(2):
        for d in (1, 2, 3):
            inbound(d, part).wait_send()
    for cp in acopies + bcopies + ccopies + dcopies + zcopies + ycopies + kcopies:
        cp.wait_send()

    @pl.loop(0, 8)
    def _(r):
        for d in (1, 3, 2):
            outbound(r, d).wait()
        keep(r).wait()


def local(orbitals, potentials, point_rows, point_cols):
    vm, dma = pltpu.VMEM, pltpu.SemaphoreType.DMA
    hbm = pl.BlockSpec(memory_space=pl.ANY)
    ix = pl.BlockSpec(memory_space=pltpu.VMEM)
    scratch = [
        vm((8, 512, 128), F32), vm((2048, 8, 256), BF), vm((8, 2048, 256), BF),
        vm((1024, 1024), BF), vm((2, 2048, 128), F32), vm((8, 256, 256), BF), vm((8, 256, 256), BF),
        vm((4, 128, 128), F32), vm((4, 128, 128), F32), vm((4, 128, 128), F32), vm((3, 128, 128), F32),
        vm((128, 128), F32), vm((7, 16, 128), F32), vm((16, 128), F32), vm((3, 16, 128), F32),
        vm((16, 128, 256), F32), vm((2048, 256), BF), vm((2048, 256), BF),
        vm((256, 2048), BF), vm((256, 2048), BF), vm((8, 256, 256), F32),
        dma((11,)), dma((2, 3)), dma((2, 3)), dma((4,)), dma((4,)), dma((3,)), dma((3,)),
        dma((7,)), dma((7,)), dma((3,)), dma((3,)), dma((7,)), dma((7,)), dma((3,)), dma((3,)),
        dma((4,)), dma((4,)), dma((8, 3)), dma((8, 3)), dma((8,)),
    ]
    out = pl.pallas_call(
        body,
        out_shape=jax.ShapeDtypeStruct((8, 64, 1024), F32),
        in_specs=[hbm, hbm, ix, ix],
        out_specs=hbm,
        scratch_shapes=scratch,
        compiler_params=pltpu.CompilerParams(
            collective_id=0, has_side_effects=True, vmem_limit_bytes=60 * 1024 * 1024),
        name="exchange",
    )(orbitals.reshape(512, 1024), potentials, point_rows.reshape(1, -1), point_cols.reshape(1, -1))
    return jnp.transpose(out, (1, 0, 2))


def solution(mesh):
    in_specs = (P("band", "grid", None), P(None, "grid", "band"), P(), P())
    out_specs = P("band", "grid", None)
    return jax.shard_map(local, mesh=mesh, in_specs=in_specs, out_specs=out_specs, check_vma=False)
```

```python
import jax
import jax.numpy as jnp
from jax import lax
from jax.experimental import pallas as pl
from jax.experimental.pallas import tpu as pltpu
from jax.sharding import PartitionSpec as P

MESH = pl.DeviceIdType.MESH
BF = jnp.bfloat16
F32 = jnp.float32
MC = 512
R1, R2 = 32, 96
LAG = 3
ORDER = (0, 1, 7, 2, 6, 3, 5, 4)
GREET = 3
IN_FIRST, IN_LAST = range(4), range(4, 8)


def split(v):
    hi = v.astype(BF)
    return hi, (v - hi.astype(F32)).astype(BF)


def body(orb, pot, rows, cols, y_out,
         orbv, vraw, vrow, amat, orecv, ohi, olo, qa, ra, qb, rb, qc, rc,
         blk, pth, ptl, ph, plo, ysend,
         lsem, in_s, in_r, a_s, a_r, b_s, b_r, c_s, c_r, d_s, d_r,
         y_s, y_r, e_s, e_r, k_s, k_r, o_s, o_r, o_l):
    x = lax.axis_index("band")
    g = lax.axis_index("grid")
    z, y, c = g // 8, (g // 2) % 4, g % 2

    def dev(xx, zz, yy, cc):
        return (xx, (zz * 4 + yy) * 2 + cc)

    def xpeer(d):
        return dev((x + d) % 4, z, y, c)

    def zpeer(d):
        return dev(x, (z + d) % 8, y, c)

    def ypeer(d):
        return dev(x, z, (y + d) % 4, c)

    partner = dev(x, z, y, 1 - c)

    def remote(src, dst, ss, rs, to):
        return pltpu.make_async_remote_copy(
            src_ref=src, dst_ref=dst, send_sem=ss, recv_sem=rs,
            device_id=to, device_id_type=MESH)

    load_orb = [pltpu.make_async_copy(orb.at[:, pl.ds(128 * t, 128)], orbv.at[t], lsem.at[t])
                for t in range(8)]
    for cp in load_orb:
        cp.start()
    load_pot = pltpu.make_async_copy(pot, vraw, lsem.at[10])
    load_pot.start()

    load_own = [pltpu.make_async_copy(
        orb.at[:, pl.ds(pl.multiple_of(256 * x + 128 * t, 128), 128)],
        orecv.at[t, pl.ds(pl.multiple_of(512 * x, 512), 512), :], lsem.at[8 + t]) for t in range(2)]
    for cp in load_own:
        cp.start()

    barrier = pltpu.get_barrier_semaphore()
    peers = ([partner] + [ypeer(d) for d in (1, 2, 3)]
             + [dev((x + dx) % 4, (z + dz) % 8, y, c) for dz in range(8) for dx in range(4) if dz or dx])
    for to in peers:
        pl.semaphore_signal(barrier, inc=1, device_id=to, device_id_type=MESH)

    for t in range(8):
        load_orb[t].wait()
        at = pl.ds(128 * t, 128)
        for r in range(8):
            hi, lo = split(orbv[t, pl.ds(r, 64, stride=8), :])
            amat[pl.ds(64 * r, 64), at] = hi
            amat[pl.ds(512 + 64 * r, 64), at] = lo

    def pick(b):
        at = pl.ds(pl.multiple_of(256 * b, 256), 256)
        hot = lax.broadcasted_iota(jnp.int32, (1024, 256), 0) == cols[:, at]
        res = jnp.dot(amat[...], jnp.where(hot, 1.0, 0.0).astype(BF), preferred_element_type=F32)
        here = rows[:, at] - 8 * g
        total = jnp.zeros((64, 256), F32)
        for r in range(8):
            part = res[64 * r:64 * r + 64] + res[512 + 64 * r:576 + 64 * r]
            total = total + jnp.where(here == r, part, 0.0)
        return jnp.concatenate([total[:, :128], total[:, 128:]], axis=0).T

    def inbound(d, part):
        t, piece = part // 4, part % 4
        to = (x + d) % 4
        return remote(
            orb.at[pl.ds(128 * piece, 128), pl.ds(pl.multiple_of(256 * to + 128 * t, 128), 128)],
            orecv.at[t, pl.ds(pl.multiple_of(512 * x + 128 * piece, 128), 128), :],
            in_s.at[part, d - 1], in_r.at[part, d - 1], xpeer(d))

    def send_inbound(parts):
        for part in parts:
            for d in (1, 3, 2):
                inbound(d, part).start()

    pend = []

    def go(cp):
        cp.start()
        pend.append(cp)
        return cp

    def rearrange(start, stop):
        @pl.loop(start, stop)
        def _(n):
            at = pl.ds(pl.multiple_of(16 * n, 16), 16)
            v = vraw[at, :, :].astype(F32)
            vrow[:, at, :] = jnp.swapaxes(v, 0, 1).astype(BF)

    acopies = []
    for i in range(4):
        qa[i] = pick((1 - c) * 4 + (y + 1 + i) % 4)
        if i == GREET:
            pl.semaphore_wait(barrier, len(peers))
            send_inbound(IN_FIRST)
        if i >= GREET:
            for k in range(len(acopies), i + 1):
                acopies.append(go(remote(qa.at[k], ra.at[k], a_s.at[k], a_r.at[k], partner)))
    bcopies = []
    for i in range(4):
        mine = pick(c * 4 + (y + 1 + i) % 4)
        acopies[i].wait_recv()
        qb[i] = mine + ra[i]
        if i < 3:
            bcopies.append(go(remote(qb.at[i], rb.at[i], b_s.at[i], b_r.at[i], ypeer(i + 1))))
    load_pot.wait()
    rearrange(0, R1)
    for cp in bcopies:
        cp.wait_recv()
    qc[...] = qb[3] + rb[0] + rb[1] + rb[2]
    ccopies = []
    for d in (4, 3, 5, 2, 6, 1, 7):
        to = (z + d) % 8
        ccopies.append(go(remote(qc.at[pl.ds(pl.multiple_of(16 * to, 16), 16), :], rc.at[d - 1],
                                 c_s.at[d - 1], c_r.at[d - 1], zpeer(d))))
    rearrange(R1, R2)
    total = qc[pl.ds(pl.multiple_of(16 * z, 16), 16), :]
    for cp in ccopies:
        cp.wait_recv()
    for d in range(7):
        total = total + rc[d]

    b = c * 4 + y
    blk[b, x, pl.ds(pl.multiple_of(16 * z, 16), 16), :] = total
    order = ORDER
    piece = blk.at[b, x, pl.ds(pl.multiple_of(16 * z, 16), 16), :]
    dcopies = {}
    for dz in order:
        for dx in (1, 3, 2, 0):
            if dz or dx:
                dcopies[dz, dx] = go(remote(piece, piece, d_s.at[dz, dx], d_r.at[dz, dx],
                                            dev((x + dx) % 4, (z + dz) % 8, y, c)))
    send_inbound(IN_LAST)
    rearrange(R2, 128)

    def group(dy, dz):
        return blk.at[c * 4 + (y + dy + 4) % 4, :,
                      pl.ds(pl.multiple_of(16 * ((z + 8 - dz) % 8), 16), 16), :]

    def cross(dy, dz):
        src = group(dy, dz)
        return go(remote(src, src, k_s.at[dy % 4, dz], k_r.at[dy % 4, dz], partner))

    up, down, relay, kcopies = {}, {}, {}, {}
    for k in range(8 + 2 * LAG):
        if k < 8:
            dz = order[k]
            for dx in range(4):
                if dz or dx:
                    dcopies[dz, dx].wait_recv()
            src = group(0, dz)
            up[dz] = go(remote(src, src, y_s.at[0, dz], y_r.at[0, dz], ypeer(1)))
            down[dz] = go(remote(src, src, y_s.at[1, dz], y_r.at[1, dz], ypeer(3)))
            kcopies[0, dz] = cross(0, dz)
        if 0 <= k - LAG < 8:
            dz = order[k - LAG]
            up[dz].wait_recv()
            if (k - LAG) % 2 == 0:
                src = group(-1, dz)
                relay[dz] = go(remote(src, src, e_s.at[dz], e_r.at[dz], ypeer(1)))
            kcopies[3, dz] = cross(-1, dz)
            down[dz].wait_recv()
            if (k - LAG) % 2 == 1:
                src = group(1, dz)
                relay[dz] = go(remote(src, src, e_s.at[dz], e_r.at[dz], ypeer(3)))
            kcopies[1, dz] = cross(1, dz)
        if 0 <= k - 2 * LAG < 8:
            dz = order[k - 2 * LAG]
            relay[dz].wait_recv()
            kcopies[2, dz] = cross(2, dz)

    for cp in load_own:
        cp.wait()
    for part in range(8):
        for d in (1, 2, 3):
            inbound(d, part).wait_recv()
    for r in range(8):
        for t in range(2):
            hi, lo = split(orecv[t, pl.ds(r, 256, stride=8), :])
            ohi[r, :, pl.ds(128 * t, 128)] = hi
            olo[r, :, pl.ds(128 * t, 128)] = lo

    eye = jnp.where(lax.broadcasted_iota(jnp.int32, (256, 256), 0)
                    == lax.broadcasted_iota(jnp.int32, (256, 256), 1), 1.0, 0.0).astype(BF)
    nt = (((1,), (1,)), ((), ()))
    low = lax.broadcasted_iota(jnp.int32, (128, 128), 1) < 64

    def unpack(n):
        first, second = [], []
        for t in range(2):
            even, odd = blk[n, 2 * t], blk[n, 2 * t + 1]
            first.append(jnp.where(low, even, pltpu.roll(odd, 64, 1)))
            second.append(jnp.where(low, pltpu.roll(even, 64, 1), odd))
        full = jnp.concatenate([jnp.concatenate(first, axis=1), jnp.concatenate(second, axis=1)], axis=0)
        at = pl.ds(pl.multiple_of(256 * n, 256), 256)
        hi, lo = split(full)
        pth[at, :] = hi
        ptl[at, :] = lo
        ph[:, at] = lax.dot_general(eye, hi, nt, preferred_element_type=F32).astype(BF)
        plo[:, at] = lax.dot_general(eye, lo, nt, preferred_element_type=F32).astype(BF)

    def outbound(r, d):
        to = (x + d) % 4
        return remote(
            ysend.at[r, pl.ds(pl.multiple_of(64 * to, 64), 64), :],
            y_out.at[r, :, pl.ds(pl.multiple_of(256 * x, 256), 256)],
            o_s.at[r, d - 1], o_r.at[r, d - 1], xpeer(d))

    def keep(r):
        return pltpu.make_async_copy(
            ysend.at[r, pl.ds(pl.multiple_of(64 * x, 64), 64), :],
            y_out.at[r, :, pl.ds(pl.multiple_of(256 * x, 256), 256)], o_l.at[r])

    def half(r, side, acc):
        oh, ol = ohi[r], olo[r]
        for n in range(1024 // MC):
            at = pl.ds(pl.multiple_of(1024 * side + MC * n, MC), MC)
            kern = (jnp.dot(pth[at, :], oh, preferred_element_type=F32)
                    + jnp.dot(ptl[at, :], oh, preferred_element_type=F32)
                    + jnp.dot(pth[at, :], ol, preferred_element_type=F32))
            wh, wl = split(kern * vrow[r, at, :].astype(F32))
            acc = (acc + jnp.dot(ph[:, at], wh, preferred_element_type=F32)
                   + jnp.dot(plo[:, at], wh, preferred_element_type=F32)
                   + jnp.dot(ph[:, at], wl, preferred_element_type=F32))
        return acc

    def finish(r, acc):
        ysend[r] = -acc
        for d in (1, 3, 2):
            outbound(r, d).start()
        keep(r).start()

    zero = jnp.zeros((256, 256), F32)
    for dy in range(4):
        unpack(c * 4 + (y + dy) % 4)
    ysend[0] = half(0, c, zero)
    for dy in (0, 1, 3, 2):
        for dz in order:
            kcopies[dy, dz].wait_recv()
        unpack((1 - c) * 4 + (y + dy) % 4)
    finish(0, half(0, 1 - c, ysend[0]))

    @pl.loop(1, 8)
    def _(r):
        finish(r, half(r, 1, half(r, 0, zero)))

    for part in range(8):
        for d in (1, 2, 3):
            inbound(d, part).wait_send()
    for cp in pend:
        cp.wait_send()

    @pl.loop(0, 8)
    def _(r):
        for d in (1, 3, 2):
            outbound(r, d).wait()
        keep(r).wait()


def relayout(src, dst):
    dst[...] = jnp.swapaxes(src[...], 0, 1)


def local(orbitals, potentials, point_rows, point_cols):
    vm, dma = pltpu.VMEM, pltpu.SemaphoreType.DMA
    hbm = pl.BlockSpec(memory_space=pl.ANY)
    ix = pl.BlockSpec(memory_space=pltpu.VMEM)
    scratch = [
        vm((8, 512, 128), F32), vm((2048, 8, 256), BF), vm((8, 2048, 256), BF),
        vm((1024, 1024), BF), vm((2, 2048, 128), F32), vm((8, 256, 256), BF), vm((8, 256, 256), BF),
        vm((4, 128, 128), F32), vm((4, 128, 128), F32), vm((4, 128, 128), F32), vm((3, 128, 128), F32),
        vm((128, 128), F32), vm((7, 16, 128), F32), vm((8, 4, 128, 128), F32),
        vm((2048, 256), BF), vm((2048, 256), BF),
        vm((256, 2048), BF), vm((256, 2048), BF), vm((8, 256, 256), F32),
        dma((11,)), dma((8, 3)), dma((8, 3)), dma((4,)), dma((4,)), dma((3,)), dma((3,)),
        dma((7,)), dma((7,)), dma((8, 4)), dma((8, 4)), dma((2, 8)), dma((2, 8)), dma((8,)), dma((8,)),
        dma((4, 8)), dma((4, 8)), dma((8, 3)), dma((8, 3)), dma((8,)),
    ]
    out = pl.pallas_call(
        body,
        out_shape=jax.ShapeDtypeStruct((8, 64, 1024), F32),
        in_specs=[hbm, hbm, ix, ix],
        out_specs=hbm,
        scratch_shapes=scratch,
        compiler_params=pltpu.CompilerParams(
            collective_id=0, has_side_effects=True, vmem_limit_bytes=60 * 1024 * 1024),
        name="exchange",
    )(orbitals.reshape(512, 1024), potentials, point_rows.reshape(1, -1), point_cols.reshape(1, -1))
    return pl.pallas_call(
        relayout,
        out_shape=jax.ShapeDtypeStruct((64, 8, 1024), F32),
        grid=(4,),
        in_specs=[pl.BlockSpec((8, 16, 1024), lambda i: (0, i, 0))],
        out_specs=pl.BlockSpec((16, 8, 1024), lambda i: (i, 0, 0)),
        name="relayout",
    )(out)


def solution(mesh):
    in_specs = (P("band", "grid", None), P(None, "grid", "band"), P(), P())
    out_specs = P("band", "grid", None)
    return jax.shard_map(local, mesh=mesh, in_specs=in_specs, out_specs=out_specs, check_vma=False)
```

```python
import jax
import jax.numpy as jnp
from jax import lax
from jax.experimental import pallas as pl
from jax.experimental.pallas import tpu as pltpu
from jax.sharding import PartitionSpec as P

MESH = pl.DeviceIdType.MESH
BF = jnp.bfloat16
F32 = jnp.float32
MC = 512
R1, R2 = 32, 64
PASSED = {2: (0,), 6: (1,), 4: (2, 3)}
LAG = 4
ORDER = (0, 1, 7, 3, 5, 2, 6, 4)
GREET = 3
IN_FIRST, IN_LAST = range(4), range(4, 8)


def split(v):
    hi = v.astype(BF)
    return hi, (v - hi.astype(F32)).astype(BF)


def body(orb, pot, rows, cols, y_out,
         orbv, vraw, vrow, amat, orecv, ohi, olo, qa, ra, qb, rb, qc, rc,
         blk, pth, ptl, ph, plo, ysend,
         lsem, in_s, in_r, a_s, a_r, b_s, b_r, c_s, c_r, d_s, d_r,
         p_s, p_r, y_s, y_r, e_s, e_r, k_s, k_r, o_s, o_r, o_l):
    x = lax.axis_index("band")
    g = lax.axis_index("grid")
    z, y, c = g // 8, (g // 2) % 4, g % 2

    def dev(xx, zz, yy, cc):
        return (xx, (zz * 4 + yy) * 2 + cc)

    def xpeer(d):
        return dev((x + d) % 4, z, y, c)

    def zpeer(d):
        return dev(x, (z + d) % 8, y, c)

    def ypeer(d):
        return dev(x, z, (y + d) % 4, c)

    partner = dev(x, z, y, 1 - c)

    def remote(src, dst, ss, rs, to):
        return pltpu.make_async_remote_copy(
            src_ref=src, dst_ref=dst, send_sem=ss, recv_sem=rs,
            device_id=to, device_id_type=MESH)

    load_orb = [pltpu.make_async_copy(orb.at[:, pl.ds(128 * t, 128)], orbv.at[t], lsem.at[t])
                for t in range(8)]
    for cp in load_orb:
        cp.start()
    load_pot = pltpu.make_async_copy(pot, vraw, lsem.at[10])
    load_pot.start()

    load_own = [pltpu.make_async_copy(
        orb.at[:, pl.ds(pl.multiple_of(256 * x + 128 * t, 128), 128)],
        orecv.at[t, pl.ds(pl.multiple_of(512 * x, 512), 512), :], lsem.at[8 + t]) for t in range(2)]
    for cp in load_own:
        cp.start()

    barrier = pltpu.get_barrier_semaphore()
    peers = ([partner] + [ypeer(d) for d in (1, 2, 3)]
             + [dev((x + dx) % 4, (z + dz) % 8, y, c) for dz in range(8) for dx in range(4)
                if (dz or dx) and (dz in (0, 1, 3, 5, 7) or dx == 0)])
    for to in peers:
        pl.semaphore_signal(barrier, inc=1, device_id=to, device_id_type=MESH)

    for t in range(8):
        load_orb[t].wait()
        at = pl.ds(128 * t, 128)
        for r in range(8):
            hi, lo = split(orbv[t, pl.ds(r, 64, stride=8), :])
            amat[pl.ds(64 * r, 64), at] = hi
            amat[pl.ds(512 + 64 * r, 64), at] = lo

    def pick(b):
        at = pl.ds(pl.multiple_of(256 * b, 256), 256)
        hot = lax.broadcasted_iota(jnp.int32, (1024, 256), 0) == cols[:, at]
        res = jnp.dot(amat[...], jnp.where(hot, 1.0, 0.0).astype(BF), preferred_element_type=F32)
        here = rows[:, at] - 8 * g
        total = jnp.zeros((64, 256), F32)
        for r in range(8):
            part = res[64 * r:64 * r + 64] + res[512 + 64 * r:576 + 64 * r]
            total = total + jnp.where(here == r, part, 0.0)
        return jnp.concatenate([total[:, :128], total[:, 128:]], axis=0).T

    def inbound(d, part):
        t, piece = part // 4, part % 4
        to = (x + d) % 4
        return remote(
            orb.at[pl.ds(128 * piece, 128), pl.ds(pl.multiple_of(256 * to + 128 * t, 128), 128)],
            orecv.at[t, pl.ds(pl.multiple_of(512 * x + 128 * piece, 128), 128), :],
            in_s.at[part, d - 1], in_r.at[part, d - 1], xpeer(d))

    def send_inbound(parts):
        for part in parts:
            for d in (1, 3, 2):
                inbound(d, part).start()

    pend = []

    def go(cp):
        cp.start()
        pend.append(cp)
        return cp

    def rearrange(start, stop):
        @pl.loop(start, stop)
        def _(n):
            at = pl.ds(pl.multiple_of(16 * n, 16), 16)
            v = vraw[at, :, :].astype(F32)
            vrow[:, at, :] = jnp.swapaxes(v, 0, 1).astype(BF)

    acopies = []
    for i in range(4):
        qa[i] = pick((1 - c) * 4 + (y + 1 + i) % 4)
        if i == GREET:
            pl.semaphore_wait(barrier, len(peers))
            send_inbound(IN_FIRST)
        if i >= GREET:
            for k in range(len(acopies), i + 1):
                acopies.append(go(remote(qa.at[k], ra.at[k], a_s.at[k], a_r.at[k], partner)))
    bcopies = []
    for i in range(4):
        mine = pick(c * 4 + (y + 1 + i) % 4)
        acopies[i].wait_recv()
        qb[i] = mine + ra[i]
        if i < 3:
            bcopies.append(go(remote(qb.at[i], rb.at[i], b_s.at[i], b_r.at[i], ypeer(i + 1))))
    load_pot.wait()
    rearrange(0, R1)
    for cp in bcopies:
        cp.wait_recv()
    qc[...] = qb[3] + rb[0] + rb[1] + rb[2]
    ccopies = []
    for d in (4, 3, 5, 2, 6, 1, 7):
        to = (z + d) % 8
        ccopies.append(go(remote(qc.at[pl.ds(pl.multiple_of(16 * to, 16), 16), :], rc.at[d - 1],
                                 c_s.at[d - 1], c_r.at[d - 1], zpeer(d))))
    rearrange(R1, R2)
    total = qc[pl.ds(pl.multiple_of(16 * z, 16), 16), :]
    for cp in ccopies:
        cp.wait_recv()
    for d in range(7):
        total = total + rc[d]

    b = c * 4 + y
    blk[b, x, pl.ds(pl.multiple_of(16 * z, 16), 16), :] = total
    order = ORDER
    piece = blk.at[b, x, pl.ds(pl.multiple_of(16 * z, 16), 16), :]
    dcopies = {}
    for dz in (0, 1, 7, 3, 5):
        for dx in (1, 3, 2, 0):
            if dz or dx:
                dcopies[dz, dx] = go(remote(piece, piece, d_s.at[dz, dx], d_r.at[dz, dx],
                                            dev((x + dx) % 4, (z + dz) % 8, y, c)))
    send_inbound(IN_LAST)
    rearrange(R2, 128)

    def group(dy, dz):
        return blk.at[c * 4 + (y + dy + 4) % 4, :,
                      pl.ds(pl.multiple_of(16 * ((z + 8 - dz) % 8), 16), 16), :]

    def cross(dy, dz):
        src = group(dy, dz)
        return go(remote(src, src, k_s.at[dy % 4, dz], k_r.at[dy % 4, dz], partner))

    up, down, relay, kcopies, passed = {}, {}, {}, {}, {}
    for k in range(8 + 2 * LAG):
        if k < 8:
            dz = order[k]
            src = group(0, dz)
            if dz in (0, 1, 3, 5, 7):
                for dx in range(4):
                    if dz or dx:
                        dcopies[dz, dx].wait_recv()
            else:
                for n in PASSED[dz]:
                    passed[n].wait_recv()
            if dz in (1, 7):
                n = 0 if dz == 1 else 1
                passed[n] = go(remote(src, src, p_s.at[n], p_r.at[n], zpeer(dz)))
            if dz in (3, 5):
                n = 2 if dz == 3 else 3
                part = src.at[pl.ds(2 * (n - 2), 2)]
                passed[n] = go(remote(part, part, p_s.at[n], p_r.at[n], zpeer(1 if dz == 3 else 7)))
            up[dz] = go(remote(src, src, y_s.at[0, dz], y_r.at[0, dz], ypeer(1)))
            down[dz] = go(remote(src, src, y_s.at[1, dz], y_r.at[1, dz], ypeer(3)))
            kcopies[0, dz] = cross(0, dz)
        if 0 <= k - LAG < 8:
            dz = order[k - LAG]
            up[dz].wait_recv()
            if (k - LAG) % 2 == 0:
                src = group(-1, dz)
                relay[dz] = go(remote(src, src, e_s.at[dz], e_r.at[dz], ypeer(1)))
            kcopies[3, dz] = cross(-1, dz)
            down[dz].wait_recv()
            if (k - LAG) % 2 == 1:
                src = group(1, dz)
                relay[dz] = go(remote(src, src, e_s.at[dz], e_r.at[dz], ypeer(3)))
            kcopies[1, dz] = cross(1, dz)
        if 0 <= k - 2 * LAG < 8:
            dz = order[k - 2 * LAG]
            relay[dz].wait_recv()
            kcopies[2, dz] = cross(2, dz)

    for cp in load_own:
        cp.wait()
    for part in range(8):
        for d in (1, 2, 3):
            inbound(d, part).wait_recv()
    for r in range(8):
        for t in range(2):
            hi, lo = split(orecv[t, pl.ds(r, 256, stride=8), :])
            ohi[r, :, pl.ds(128 * t, 128)] = hi
            olo[r, :, pl.ds(128 * t, 128)] = lo

    eye = jnp.where(lax.broadcasted_iota(jnp.int32, (256, 256), 0)
                    == lax.broadcasted_iota(jnp.int32, (256, 256), 1), 1.0, 0.0).astype(BF)
    nt = (((1,), (1,)), ((), ()))
    low = lax.broadcasted_iota(jnp.int32, (128, 128), 1) < 64

    def unpack(n):
        first, second = [], []
        for t in range(2):
            even, odd = blk[n, 2 * t], blk[n, 2 * t + 1]
            first.append(jnp.where(low, even, pltpu.roll(odd, 64, 1)))
            second.append(jnp.where(low, pltpu.roll(even, 64, 1), odd))
        full = jnp.concatenate([jnp.concatenate(first, axis=1), jnp.concatenate(second, axis=1)], axis=0)
        at = pl.ds(pl.multiple_of(256 * n, 256), 256)
        hi, lo = split(full)
        pth[at, :] = hi
        ptl[at, :] = lo
        ph[:, at] = lax.dot_general(eye, hi, nt, preferred_element_type=F32).astype(BF)
        plo[:, at] = lax.dot_general(eye, lo, nt, preferred_element_type=F32).astype(BF)

    def outbound(r, d):
        to = (x + d) % 4
        return remote(
            ysend.at[r, pl.ds(pl.multiple_of(64 * to, 64), 64), :],
            y_out.at[r, :, pl.ds(pl.multiple_of(256 * x, 256), 256)],
            o_s.at[r, d - 1], o_r.at[r, d - 1], xpeer(d))

    def keep(r):
        return pltpu.make_async_copy(
            ysend.at[r, pl.ds(pl.multiple_of(64 * x, 64), 64), :],
            y_out.at[r, :, pl.ds(pl.multiple_of(256 * x, 256), 256)], o_l.at[r])

    def half(r, side, acc):
        oh, ol = ohi[r], olo[r]
        for n in range(1024 // MC):
            at = pl.ds(pl.multiple_of(1024 * side + MC * n, MC), MC)
            kern = (jnp.dot(pth[at, :], oh, preferred_element_type=F32)
                    + jnp.dot(ptl[at, :], oh, preferred_element_type=F32)
                    + jnp.dot(pth[at, :], ol, preferred_element_type=F32))
            wh, wl = split(kern * vrow[r, at, :].astype(F32))
            acc = (acc + jnp.dot(ph[:, at], wh, preferred_element_type=F32)
                   + jnp.dot(plo[:, at], wh, preferred_element_type=F32)
                   + jnp.dot(ph[:, at], wl, preferred_element_type=F32))
        return acc

    def finish(r, acc):
        ysend[r] = -acc
        for d in (1, 3, 2):
            outbound(r, d).start()
        keep(r).start()

    zero = jnp.zeros((256, 256), F32)
    for dy in range(4):
        unpack(c * 4 + (y + dy) % 4)
    ysend[0] = half(0, c, zero)
    for dy in (0, 1, 3, 2):
        for dz in order:
            kcopies[dy, dz].wait_recv()
        unpack((1 - c) * 4 + (y + dy) % 4)
    finish(0, half(0, 1 - c, ysend[0]))

    @pl.loop(1, 8)
    def _(r):
        finish(r, half(r, 1, half(r, 0, zero)))

    for part in range(8):
        for d in (1, 2, 3):
            inbound(d, part).wait_send()
    for cp in pend:
        cp.wait_send()

    @pl.loop(0, 8)
    def _(r):
        for d in (1, 3, 2):
            outbound(r, d).wait()
        keep(r).wait()


def relayout(src, dst, got, done, s_in, s_out):
    ins = [pltpu.make_async_copy(src.at[:, pl.ds(8 * i, 8), :], got.at[i], s_in.at[i]) for i in range(8)]
    outs = [pltpu.make_async_copy(done.at[i], dst.at[pl.ds(8 * i, 8)], s_out.at[i]) for i in range(8)]
    for cp in ins:
        cp.start()
    for i in range(8):
        ins[i].wait()
        done[i] = jnp.swapaxes(got[i], 0, 1)
        outs[i].start()
    for cp in outs:
        cp.wait()


def local(orbitals, potentials, point_rows, point_cols):
    vm, dma = pltpu.VMEM, pltpu.SemaphoreType.DMA
    hbm = pl.BlockSpec(memory_space=pl.ANY)
    ix = pl.BlockSpec(memory_space=pltpu.VMEM)
    scratch = [
        vm((8, 512, 128), F32), vm((2048, 8, 256), BF), vm((8, 2048, 256), BF),
        vm((1024, 1024), BF), vm((2, 2048, 128), F32), vm((8, 256, 256), BF), vm((8, 256, 256), BF),
        vm((4, 128, 128), F32), vm((4, 128, 128), F32), vm((4, 128, 128), F32), vm((3, 128, 128), F32),
        vm((128, 128), F32), vm((7, 16, 128), F32), vm((8, 4, 128, 128), F32),
        vm((2048, 256), BF), vm((2048, 256), BF),
        vm((256, 2048), BF), vm((256, 2048), BF), vm((8, 256, 256), F32),
        dma((11,)), dma((8, 3)), dma((8, 3)), dma((4,)), dma((4,)), dma((3,)), dma((3,)),
        dma((7,)), dma((7,)), dma((8, 4)), dma((8, 4)), dma((4,)), dma((4,)), dma((2, 8)), dma((2, 8)), dma((8,)), dma((8,)),
        dma((4, 8)), dma((4, 8)), dma((8, 3)), dma((8, 3)), dma((8,)),
    ]
    out = pl.pallas_call(
        body,
        out_shape=jax.ShapeDtypeStruct((8, 64, 1024), F32),
        in_specs=[hbm, hbm, ix, ix],
        out_specs=hbm,
        scratch_shapes=scratch,
        compiler_params=pltpu.CompilerParams(
            collective_id=0, has_side_effects=True, vmem_limit_bytes=60 * 1024 * 1024),
        name="exchange",
    )(orbitals.reshape(512, 1024), potentials, point_rows.reshape(1, -1), point_cols.reshape(1, -1))
    return pl.pallas_call(
        relayout,
        out_shape=jax.ShapeDtypeStruct((64, 8, 1024), F32),
        in_specs=[hbm],
        out_specs=hbm,
        scratch_shapes=[vm((8, 8, 8, 1024), F32), vm((8, 8, 8, 1024), F32), dma((8,)), dma((8,))],
        compiler_params=pltpu.CompilerParams(vmem_limit_bytes=60 * 1024 * 1024),
        name="relayout",
    )(out)


def solution(mesh):
    in_specs = (P("band", "grid", None), P(None, "grid", "band"), P(), P())
    out_specs = P("band", "grid", None)
    return jax.shard_map(local, mesh=mesh, in_specs=in_specs, out_specs=out_specs, check_vma=False)
```

```python
import jax
import jax.numpy as jnp
from jax import lax
from jax.experimental import pallas as pl
from jax.experimental.pallas import tpu as pltpu
from jax.sharding import PartitionSpec as P

MESH = pl.DeviceIdType.MESH
BF = jnp.bfloat16
F32 = jnp.float32
MC = 512
R1, R2 = 32, 64
PASSED = {2: (0,), 6: (1,), 4: (2, 3)}
LAG = 4
ORDER = (0, 1, 7, 3, 5, 2, 6, 4)
GREET = 3
IN_FIRST, IN_LAST = range(4), range(4, 8)


def split(v):
    hi = v.astype(BF)
    return hi, (v - hi.astype(F32)).astype(BF)


def body(orb, pot, rows, cols, y_out,
         orbv, vraw, vrow, amat, orecv, ohi, olo, qa, ra, qb, rb, qc, rc,
         blk, pth, ptl, ph, plo, ysend,
         lsem, in_s, in_r, a_s, a_r, b_s, b_r, c_s, c_r, d_s, d_r,
         p_s, p_r, y_s, y_r, e_s, e_r, k_s, k_r, o_s, o_r, o_l):
    x = lax.axis_index("band")
    g = lax.axis_index("grid")
    z, y, c = g // 8, (g // 2) % 4, g % 2

    def dev(xx, zz, yy, cc):
        return (xx, (zz * 4 + yy) * 2 + cc)

    def xpeer(d):
        return dev((x + d) % 4, z, y, c)

    def zpeer(d):
        return dev(x, (z + d) % 8, y, c)

    def ypeer(d):
        return dev(x, z, (y + d) % 4, c)

    partner = dev(x, z, y, 1 - c)

    def remote(src, dst, ss, rs, to):
        return pltpu.make_async_remote_copy(
            src_ref=src, dst_ref=dst, send_sem=ss, recv_sem=rs,
            device_id=to, device_id_type=MESH)

    load_orb = [pltpu.make_async_copy(orb.at[:, pl.ds(128 * t, 128)], orbv.at[t], lsem.at[t])
                for t in range(8)]
    for cp in load_orb:
        cp.start()
    load_pot = pltpu.make_async_copy(pot, vraw, lsem.at[10])
    load_pot.start()

    load_own = [pltpu.make_async_copy(
        orb.at[:, pl.ds(pl.multiple_of(256 * x + 128 * t, 128), 128)],
        orecv.at[t, pl.ds(pl.multiple_of(512 * x, 512), 512), :], lsem.at[8 + t]) for t in range(2)]
    for cp in load_own:
        cp.start()

    barrier = pltpu.get_barrier_semaphore()
    peers = ([partner] + [ypeer(d) for d in (1, 2, 3)]
             + [dev((x + dx) % 4, (z + dz) % 8, y, c) for dz in range(8) for dx in range(4)
                if (dz or dx) and (dz in (0, 1, 3, 5, 7) or dx == 0)])
    for to in peers:
        pl.semaphore_signal(barrier, inc=1, device_id=to, device_id_type=MESH)

    for t in range(8):
        load_orb[t].wait()
        at = pl.ds(128 * t, 128)
        for r in range(8):
            hi, lo = split(orbv[t, pl.ds(r, 64, stride=8), :])
            amat[pl.ds(64 * r, 64), at] = hi
            amat[pl.ds(512 + 64 * r, 64), at] = lo

    def pick(b):
        at = pl.ds(pl.multiple_of(256 * b, 256), 256)
        hot = lax.broadcasted_iota(jnp.int32, (1024, 256), 0) == cols[:, at]
        res = jnp.dot(amat[...], jnp.where(hot, 1.0, 0.0).astype(BF), preferred_element_type=F32)
        here = rows[:, at] - 8 * g
        total = jnp.zeros((64, 256), F32)
        for r in range(8):
            part = res[64 * r:64 * r + 64] + res[512 + 64 * r:576 + 64 * r]
            total = total + jnp.where(here == r, part, 0.0)
        return jnp.concatenate([total[:, :128], total[:, 128:]], axis=0).T

    def inbound(d, part):
        t, piece = part // 4, part % 4
        to = (x + d) % 4
        return remote(
            orb.at[pl.ds(128 * piece, 128), pl.ds(pl.multiple_of(256 * to + 128 * t, 128), 128)],
            orecv.at[t, pl.ds(pl.multiple_of(512 * x + 128 * piece, 128), 128), :],
            in_s.at[part, d - 1], in_r.at[part, d - 1], xpeer(d))

    def send_inbound(parts):
        for part in parts:
            for d in (1, 3, 2):
                inbound(d, part).start()

    pend = []

    def go(cp):
        cp.start()
        pend.append(cp)
        return cp

    def rearrange(start, stop):
        @pl.loop(start, stop)
        def _(n):
            at = pl.ds(pl.multiple_of(16 * n, 16), 16)
            v = vraw[at, :, :].astype(F32)
            vrow[:, at, :] = jnp.swapaxes(v, 0, 1).astype(BF)

    acopies = []
    for i in range(4):
        qa[i] = pick((1 - c) * 4 + (y + 1 + i) % 4)
        if i == GREET:
            pl.semaphore_wait(barrier, len(peers))
            send_inbound(IN_FIRST)
        if i >= GREET:
            for k in range(len(acopies), i + 1):
                acopies.append(go(remote(qa.at[k], ra.at[k], a_s.at[k], a_r.at[k], partner)))
    bcopies = []
    for i in range(4):
        mine = pick(c * 4 + (y + 1 + i) % 4)
        acopies[i].wait_recv()
        qb[i] = mine + ra[i]
        if i < 3:
            bcopies.append(go(remote(qb.at[i], rb.at[i], b_s.at[i], b_r.at[i], ypeer(i + 1))))
    load_pot.wait()
    rearrange(0, R1)
    for cp in bcopies:
        cp.wait_recv()
    qc[...] = qb[3] + rb[0] + rb[1] + rb[2]
    ccopies = []
    for d in (4, 3, 5, 2, 6, 1, 7):
        to = (z + d) % 8
        ccopies.append(go(remote(qc.at[pl.ds(pl.multiple_of(16 * to, 16), 16), :], rc.at[d - 1],
                                 c_s.at[d - 1], c_r.at[d - 1], zpeer(d))))
    rearrange(R1, R2)
    total = qc[pl.ds(pl.multiple_of(16 * z, 16), 16), :]
    for cp in ccopies:
        cp.wait_recv()
    for d in range(7):
        total = total + rc[d]

    b = c * 4 + y
    blk[b, x, pl.ds(pl.multiple_of(16 * z, 16), 16), :] = total
    order = ORDER
    piece = blk.at[b, x, pl.ds(pl.multiple_of(16 * z, 16), 16), :]
    dcopies = {}
    for dz in (0, 1, 7, 3, 5):
        for dx in (1, 3, 2, 0):
            if dz or dx:
                dcopies[dz, dx] = go(remote(piece, piece, d_s.at[dz, dx], d_r.at[dz, dx],
                                            dev((x + dx) % 4, (z + dz) % 8, y, c)))
    send_inbound(IN_LAST)
    rearrange(R2, 128)

    def group(dy, dz):
        return blk.at[c * 4 + (y + dy + 4) % 4, :,
                      pl.ds(pl.multiple_of(16 * ((z + 8 - dz) % 8), 16), 16), :]

    def cross(dy, dz):
        src = group(dy, dz)
        return go(remote(src, src, k_s.at[dy % 4, dz], k_r.at[dy % 4, dz], partner))

    eye = jnp.where(lax.broadcasted_iota(jnp.int32, (256, 256), 0)
                    == lax.broadcasted_iota(jnp.int32, (256, 256), 1), 1.0, 0.0).astype(BF)
    nt = (((1,), (1,)), ((), ()))
    low = lax.broadcasted_iota(jnp.int32, (128, 128), 1) < 64

    def unpack(n):
        first, second = [], []
        for t in range(2):
            even, odd = blk[n, 2 * t], blk[n, 2 * t + 1]
            first.append(jnp.where(low, even, pltpu.roll(odd, 64, 1)))
            second.append(jnp.where(low, pltpu.roll(even, 64, 1), odd))
        full = jnp.concatenate([jnp.concatenate(first, axis=1), jnp.concatenate(second, axis=1)], axis=0)
        at = pl.ds(pl.multiple_of(256 * n, 256), 256)
        hi, lo = split(full)
        pth[at, :] = hi
        ptl[at, :] = lo
        ph[:, at] = lax.dot_general(eye, hi, nt, preferred_element_type=F32).astype(BF)
        plo[:, at] = lax.dot_general(eye, lo, nt, preferred_element_type=F32).astype(BF)

    def contrib(r, start, size, acc):
        oh, ol = ohi[r], olo[r]
        at = pl.ds(pl.multiple_of(start, size), size)
        kern = (jnp.dot(pth[at, :], oh, preferred_element_type=F32)
                + jnp.dot(ptl[at, :], oh, preferred_element_type=F32)
                + jnp.dot(pth[at, :], ol, preferred_element_type=F32))
        wh, wl = split(kern * vrow[r, at, :].astype(F32))
        return (acc + jnp.dot(ph[:, at], wh, preferred_element_type=F32)
                + jnp.dot(plo[:, at], wh, preferred_element_type=F32)
                + jnp.dot(ph[:, at], wl, preferred_element_type=F32))

    def first(n):
        unpack(n)
        ysend[0] = contrib(0, 256 * n, 256, ysend[0])

    def split_inbound(t):
        load_own[t].wait()
        for part in range(4 * t, 4 * t + 4):
            for d in (1, 2, 3):
                inbound(d, part).wait_recv()
        for r in range(8):
            hi, lo = split(orecv[t, pl.ds(r, 256, stride=8), :])
            ohi[r, :, pl.ds(128 * t, 128)] = hi
            olo[r, :, pl.ds(128 * t, 128)] = lo

    split_inbound(0)
    ysend[0] = jnp.zeros((256, 256), F32)

    up, down, relay, kcopies, passed = {}, {}, {}, {}, {}
    for k in range(8 + 2 * LAG):
        if k < 8:
            dz = order[k]
            src = group(0, dz)
            if dz in (0, 1, 3, 5, 7):
                for dx in range(4):
                    if dz or dx:
                        dcopies[dz, dx].wait_recv()
            else:
                for n in PASSED[dz]:
                    passed[n].wait_recv()
            if dz in (1, 7):
                n = 0 if dz == 1 else 1
                passed[n] = go(remote(src, src, p_s.at[n], p_r.at[n], zpeer(dz)))
            if dz in (3, 5):
                n = 2 if dz == 3 else 3
                part = src.at[pl.ds(2 * (n - 2), 2)]
                passed[n] = go(remote(part, part, p_s.at[n], p_r.at[n], zpeer(1 if dz == 3 else 7)))
            up[dz] = go(remote(src, src, y_s.at[0, dz], y_r.at[0, dz], ypeer(1)))
            down[dz] = go(remote(src, src, y_s.at[1, dz], y_r.at[1, dz], ypeer(3)))
            kcopies[0, dz] = cross(0, dz)
        if 0 <= k - LAG < 8:
            dz = order[k - LAG]
            up[dz].wait_recv()
            if (k - LAG) % 2 == 0:
                src = group(-1, dz)
                relay[dz] = go(remote(src, src, e_s.at[dz], e_r.at[dz], ypeer(1)))
            kcopies[3, dz] = cross(-1, dz)
            down[dz].wait_recv()
            if (k - LAG) % 2 == 1:
                src = group(1, dz)
                relay[dz] = go(remote(src, src, e_s.at[dz], e_r.at[dz], ypeer(3)))
            kcopies[1, dz] = cross(1, dz)
        if 0 <= k - 2 * LAG < 8:
            dz = order[k - 2 * LAG]
            relay[dz].wait_recv()
            kcopies[2, dz] = cross(2, dz)
        if k == 7 + 2 * LAG:
            split_inbound(1)
            for dy in (0, 1, 3):
                first(c * 4 + (y + dy) % 4)

    def outbound(r, d):
        to = (x + d) % 4
        return remote(
            ysend.at[r, pl.ds(pl.multiple_of(64 * to, 64), 64), :],
            y_out.at[r, :, pl.ds(pl.multiple_of(256 * x, 256), 256)],
            o_s.at[r, d - 1], o_r.at[r, d - 1], xpeer(d))

    def keep(r):
        return pltpu.make_async_copy(
            ysend.at[r, pl.ds(pl.multiple_of(64 * x, 64), 64), :],
            y_out.at[r, :, pl.ds(pl.multiple_of(256 * x, 256), 256)], o_l.at[r])

    def finish(r, acc):
        ysend[r] = -acc
        for d in (1, 3, 2):
            outbound(r, d).start()
        keep(r).start()

    first(c * 4 + (y + 2) % 4)
    for dy in (0, 1, 3, 2):
        for dz in order:
            kcopies[dy, dz].wait_recv()
        first((1 - c) * 4 + (y + dy) % 4)
    finish(0, ysend[0])

    @pl.loop(1, 8)
    def _(r):
        acc = jnp.zeros((256, 256), F32)
        for n in range(2048 // MC):
            acc = contrib(r, MC * n, MC, acc)
        finish(r, acc)

    for part in range(8):
        for d in (1, 2, 3):
            inbound(d, part).wait_send()
    for cp in pend:
        cp.wait_send()

    @pl.loop(0, 8)
    def _(r):
        for d in (1, 3, 2):
            outbound(r, d).wait()
        keep(r).wait()


def relayout(src, dst, got, done, s_in, s_out):
    ins = [pltpu.make_async_copy(src.at[:, pl.ds(8 * i, 8), :], got.at[i], s_in.at[i]) for i in range(8)]
    outs = [pltpu.make_async_copy(done.at[i], dst.at[pl.ds(8 * i, 8)], s_out.at[i]) for i in range(8)]
    for cp in ins:
        cp.start()
    for i in range(8):
        ins[i].wait()
        done[i] = jnp.swapaxes(got[i], 0, 1)
        outs[i].start()
    for cp in outs:
        cp.wait()


def local(orbitals, potentials, point_rows, point_cols):
    vm, dma = pltpu.VMEM, pltpu.SemaphoreType.DMA
    hbm = pl.BlockSpec(memory_space=pl.ANY)
    ix = pl.BlockSpec(memory_space=pltpu.VMEM)
    scratch = [
        vm((8, 512, 128), F32), vm((2048, 8, 256), BF), vm((8, 2048, 256), BF),
        vm((1024, 1024), BF), vm((2, 2048, 128), F32), vm((8, 256, 256), BF), vm((8, 256, 256), BF),
        vm((4, 128, 128), F32), vm((4, 128, 128), F32), vm((4, 128, 128), F32), vm((3, 128, 128), F32),
        vm((128, 128), F32), vm((7, 16, 128), F32), vm((8, 4, 128, 128), F32),
        vm((2048, 256), BF), vm((2048, 256), BF),
        vm((256, 2048), BF), vm((256, 2048), BF), vm((8, 256, 256), F32),
        dma((11,)), dma((8, 3)), dma((8, 3)), dma((4,)), dma((4,)), dma((3,)), dma((3,)),
        dma((7,)), dma((7,)), dma((8, 4)), dma((8, 4)), dma((4,)), dma((4,)), dma((2, 8)), dma((2, 8)), dma((8,)), dma((8,)),
        dma((4, 8)), dma((4, 8)), dma((8, 3)), dma((8, 3)), dma((8,)),
    ]
    out = pl.pallas_call(
        body,
        out_shape=jax.ShapeDtypeStruct((8, 64, 1024), F32),
        in_specs=[hbm, hbm, ix, ix],
        out_specs=hbm,
        scratch_shapes=scratch,
        compiler_params=pltpu.CompilerParams(
            collective_id=0, has_side_effects=True, vmem_limit_bytes=60 * 1024 * 1024),
        name="exchange",
    )(orbitals.reshape(512, 1024), potentials, point_rows.reshape(1, -1), point_cols.reshape(1, -1))
    return pl.pallas_call(
        relayout,
        out_shape=jax.ShapeDtypeStruct((64, 8, 1024), F32),
        in_specs=[hbm],
        out_specs=hbm,
        scratch_shapes=[vm((8, 8, 8, 1024), F32), vm((8, 8, 8, 1024), F32), dma((8,)), dma((8,))],
        compiler_params=pltpu.CompilerParams(vmem_limit_bytes=60 * 1024 * 1024),
        name="relayout",
    )(out)


def solution(mesh):
    in_specs = (P("band", "grid", None), P(None, "grid", "band"), P(), P())
    out_specs = P("band", "grid", None)
    return jax.shard_map(local, mesh=mesh, in_specs=in_specs, out_specs=out_specs, check_vma=False)
```
